32 devices in a mesh: gx: 4 (over z), gy: 8 (over y, x, core).
Axes of the slice: x: 2, y: 2, z: 4, core: 2. Of those that a mesh axis runs over, the one named last changes fastest.
Arguments:
- centres: bfloat16 [131072, 256], P(('gx', 'gy')), may hold values from -20 to 20
- weights: float32 [16, 131072], P(None, ('gx', 'gy')), may hold values from -1 to 1
- targets: float32 [16, 256], P(None, ('gx', 'gy')), may hold values from -6 to 6
- batch_index: int32 [256], P(('gx', 'gy')), may hold values from 0 to 131071, as said below
- nystrom_index: int32 [2048], P(('gx', 'gy')), may hold values from 0 to 131071, as said below
- eigvecs: float32 [2048, 128], P(('gx', 'gy')), may hold values from -0.125 to 0.125
- scales: float32 [128], replicated, may hold values from 0.2 to 2
Outputs:
- residual: float32 [16, 256], P(None, ('gx', 'gy'))
- block_correction: float32 [16, 2048], P(None, ('gx', 'gy'))
The draws below stay inside these ranges and needn't reach their ends.
Inputs may be any that keep to these rules, and one draw needn't show every extreme that they name: `batch_index`: the entries at positions j * 8 to (j + 1) * 8 - 1 name centres j * 4096 to (j + 1) * 4096 - 1, all different. `nystrom_index`: the entries at positions j * 64 to (j + 1) * 64 - 1 name centres j * 4096 to (j + 1) * 4096 - 1, all different.
All inputs are finite; a program needn't handle non-finite values.
Results may differ from the reference program's by a relative error of at most 0.0003.
Values may be sent and summed in bfloat16 or wider, within the bound.
A program may use at most 192 MiB of HBM per device.

```python
import math
import jax
import jax.numpy as jnp
from jax import lax

D = 256
OUTPUTS = 16
EIGEN = 128
P_DEV = 4096
B_DEV = 8
S_DEV = 64
CENTRES = 131072
BATCH = 256
NYSTROM = 2048


def draw_centres(key, part):
    keys = jax.random.split(jax.random.fold_in(key, 11), 6)
    groups = jax.random.randint(keys[0], (CENTRES,), 0, 64)
    mixing = jax.random.normal(keys[1], (16, D), jnp.float32) * 0.25
    latent_noise = jax.random.normal(keys[2], (CENTRES, 16), jnp.float32)
    noise = jnp.clip(jax.random.normal(keys[3], (CENTRES, D), jnp.float32), -5.0, 5.0)
    means = jax.random.normal(keys[4], (64, 16), jnp.float32) * 3.0
    spread = jnp.exp(jax.random.uniform(keys[5], (CENTRES, 1), jnp.float32, jnp.log(0.5), jnp.log(1.5)))
    latent = jnp.take(means, groups, axis=0) + spread * latent_noise
    values = jnp.dot(latent, mixing, precision=lax.Precision.HIGHEST) + noise
    return jnp.clip(values, -20.0, 20.0).astype(jnp.bfloat16)


def index_pair(key):
    device_count = CENTRES // P_DEV
    keys = jax.random.split(jax.random.fold_in(key, 23), device_count)

    def one_device(device_key):
        order = jax.random.permutation(device_key, P_DEV).astype(jnp.int32)
        return (order[:B_DEV], order[B_DEV:B_DEV + S_DEV])
    batch_part, block_part = jax.vmap(one_device)(keys)
    offsets = (jnp.arange(device_count, dtype=jnp.int32) * P_DEV)[:, None]
    return ((batch_part + offsets).reshape(-1), (block_part + offsets).reshape(-1))


def draw_batch_index(key, part):
    return index_pair(key)[0]


def draw_nystrom_index(key, part):
    return index_pair(key)[1]


def levels(stream_key, extent, cuts, low, top_value):
    factor_of = 1.0
    for dim, shards_of in cuts:
        heights = jax.random.uniform(jax.random.fold_in(jax.random.fold_in(stream_key, 6), dim), (shards_of,), jnp.float32, low / len(cuts), top_value / len(cuts))
        factor_of = factor_of * jnp.repeat(jnp.exp(heights), extent[dim] // shards_of).reshape((-1,) + (1,) * (len(extent) - 1 - dim))
    return factor_of


def normal_values(own_key, extent, scale, reach, cuts=(), kind=jnp.bfloat16):
    values = jax.random.normal(own_key, extent, jnp.float32) * scale
    if len(cuts) > 0:
        values = levels(own_key, extent, cuts, -0.22, 0.18) * values
    return jnp.clip(values, min=-reach, max=reach).astype(kind)


def setup_inputs(seed: int = 0) -> dict:
    key_of = jax.random.split(jax.random.key(seed), 8)
    return {
        "centres": draw_centres(jax.random.fold_in(key_of[7], 71), 0),
        "weights": normal_values(key_of[1], (OUTPUTS, CENTRES), (max(CENTRES // 4096, 1)) ** -0.5, 1.0, ((1, 32),), jnp.float32),
        "targets": normal_values(key_of[2], (OUTPUTS, BATCH), 1.0, 6.0, ((1, 32),), jnp.float32),
        "batch_index": draw_batch_index(jax.random.fold_in(key_of[7], 71), 0),
        "nystrom_index": draw_nystrom_index(jax.random.fold_in(key_of[7], 71), 0),
        "eigvecs": normal_values(key_of[5], (NYSTROM, EIGEN), NYSTROM ** -0.5, 0.125, ((0, 32),), jnp.float32),
        "scales": jnp.clip(jnp.exp(jax.random.uniform(key_of[6], (EIGEN,), jnp.float32, math.log(0.2), math.log(2.0))), 0.2, 2.0),
    }


def kernel_matrix(points, others):
    width = float(points.shape[1]) ** 0.5
    point_norm = lax.optimization_barrier(jnp.sum(points.astype(jnp.float32) ** 2, axis=1))
    other_norm = lax.optimization_barrier(jnp.sum(others.astype(jnp.float32) ** 2, axis=1))
    inner = jnp.dot(points, others.T, preferred_element_type=jnp.float32)
    squared = point_norm[:, None] + other_norm[None, :] - 2.0 * inner
    return jnp.exp(-jnp.sqrt(jnp.maximum(squared, 1.0)) / width)

def reference(centres, weights, targets, batch_index, nystrom_index, eigvecs, scales):
    batch_points = jnp.take(centres, batch_index, axis=0)
    block_count = CENTRES // P_DEV

    def accumulate(step_no, total):
        first = (step_no * P_DEV).astype(jnp.int32)
        others = lax.dynamic_slice_in_dim(centres, first, P_DEV, 0)
        coeffs = lax.dynamic_slice_in_dim(weights, first, P_DEV, 1)
        tile = kernel_matrix(batch_points, others)
        return total + jnp.dot(coeffs, tile.T, precision=lax.Precision.HIGHEST)
    prediction = lax.fori_loop(0, block_count, accumulate, jnp.zeros((OUTPUTS, BATCH), jnp.float32))
    residual = prediction - targets
    block_points = jnp.take(centres, nystrom_index, axis=0)
    block_kernel = kernel_matrix(block_points, batch_points)
    along = jnp.dot(block_kernel, residual.T, precision=lax.Precision.HIGHEST)
    projection = jnp.dot(eigvecs.T, along, precision=lax.Precision.HIGHEST)
    correction = jnp.dot(eigvecs * scales[None, :], projection, precision=lax.Precision.HIGHEST)
    return (residual, correction.T)
```

```python
import functools
import math

import jax
import jax.numpy as jnp
from jax import lax
from jax.experimental import pallas as pl
from jax.experimental.pallas import tpu as pltpu
from jax.sharding import PartitionSpec as P

F32 = jnp.float32
BF16 = jnp.bfloat16
HIGHEST = lax.Precision.HIGHEST
NT = (((1,), (1,)), ((), ()))
MESH = pl.DeviceIdType.MESH


def nt(a, b, precision=None):
    return lax.dot_general(a, b, NT, precision=precision, preferred_element_type=F32)


def split(x):
    high = x.astype(BF16)
    return high, (x - high.astype(F32)).astype(BF16)


def kernel(
    nx, ny,
    bidx, nidx, targets, eig, scales, weights_hbm, centres_hbm,
    res_out, corr_out,
    cen, wv, w2, nj, rows_buf, rowsm, nb, acc, khi, klo,
    mt_loc, mt_recv, mt_all, p_loc, p_recv, r_all,
    cen_sem, w_sem, send_sems, recv_sems,
):
    n = nx * ny
    gx, gy = lax.axis_index("gx"), lax.axis_index("gy")
    me = gx * ny + gy
    count, dim = cen.shape
    outputs = wv.shape[0]
    per = rows_buf.shape[1]
    batch = n * per
    lanes = per * outputs
    block = eig.shape[0]
    step_j = khi.shape[1]
    step_b = khi.shape[0]
    rate = -math.log2(math.e) / float(dim) ** 0.5

    cen_copies = []
    parts = cen_sem.shape[0]
    size = count // parts
    for part in range(parts):
        at = pl.ds(part * size, size)
        copy = pltpu.make_async_copy(centres_hbm.at[at], cen.at[at], cen_sem.at[part])
        copy.start()
        cen_copies.append(copy)
    w_copy = pltpu.make_async_copy(weights_hbm, wv, w_sem)
    w_copy.start()

    barrier = pltpu.get_barrier_semaphore()

    def other(k):
        t = lax.rem(me + k, n)
        return t, (lax.div(t, ny), lax.rem(t, ny))

    def greet(k, carry):
        _, where = other(k)
        pl.semaphore_signal(barrier, inc=1, device_id=where, device_id_type=MESH)
        return carry

    lax.fori_loop(1, n, greet, 0)

    def send_all(phase, source, target):
        def one(k, carry):
            t, where = other(k)
            pltpu.make_async_remote_copy(
                src_ref=source(t), dst_ref=target.at[me],
                send_sem=send_sems.at[phase], recv_sem=recv_sems.at[phase],
                device_id=where, device_id_type=MESH,
            ).start()
            return carry

        lax.fori_loop(1, n, one, 0)

    def wait_bytes(buf, sem):
        view = buf.at[pl.ds(0, n - 1)]
        pltpu.make_async_copy(view, view, sem).wait()

    first = me * count

    def column(ref):
        length = ref.shape[1]
        local = (ref[...] - first).astype(F32)
        row = lax.broadcasted_iota(jnp.int32, (length, length), 0)
        col = lax.broadcasted_iota(jnp.int32, (length, length), 1)
        return jnp.sum(jnp.where(row == col, local, 0.0), axis=1, keepdims=True)

    wanted = jnp.concatenate([column(bidx), column(nidx)], axis=0)
    picked = jnp.zeros((per + block, dim), F32)
    for part in range(parts):
        cen_copies[part].wait()
        spot = lax.broadcasted_iota(jnp.int32, (per + block, size), 1) + part * size
        hot = jnp.where(spot.astype(F32) == wanted, 1.0, 0.0).astype(BF16)
        picked = picked + jnp.dot(hot, cen[part * size:(part + 1) * size, :], preferred_element_type=F32)
    rows_buf[me] = picked[:per].astype(BF16)
    pl.semaphore_wait(barrier, n - 1)
    send_all(0, lambda t: rows_buf.at[me], rows_buf)

    blk = picked[per:]
    ones_f = jnp.ones((8, dim), F32)
    blk_norm = nt(ones_f, blk * blk, HIGHEST)[:1]
    blk = blk.astype(BF16)
    ones_b = jnp.ones((8, dim), BF16)

    def norms(i, carry):
        at = pl.ds(pl.multiple_of(i * 512, 512), 512)
        v = cen[at, :].astype(F32)
        high, low = split(v * v)
        nj[:, at] = nt(ones_b, high) + nt(ones_b, low)
        return carry

    lax.fori_loop(0, count // 512, norms, 0)
    w_copy.wait()
    whigh, wlow = split(wv[...])
    for rep in range(per):
        w2[rep * outputs:(rep + 1) * outputs, :] = whigh
        w2[lanes + rep * outputs:lanes + (rep + 1) * outputs, :] = wlow
    scaled = eig[...] * scales[...]
    o_row = lax.broadcasted_iota(jnp.int32, (outputs, lanes), 0)
    o_col = lax.broadcasted_iota(jnp.int32, (outputs, lanes), 1)
    o_mask = jnp.where(lax.rem(o_col, outputs) == o_row, 1.0, 0.0)
    b_row = lax.broadcasted_iota(jnp.int32, (per, lanes), 0)
    b_col = lax.broadcasted_iota(jnp.int32, (per, lanes), 1)
    b_mask = jnp.where(lax.div(b_col, outputs) == b_row, 1.0, 0.0)
    tgt = jnp.dot(targets[...], b_mask, precision=HIGHEST, preferred_element_type=F32)
    tgt = jnp.sum(tgt * o_mask, axis=0, keepdims=True)

    wait_bytes(rows_buf, recv_sems.at[0])
    rows = rows_buf[...].astype(F32).reshape(batch, dim)
    row_norm = jnp.sum(rows * rows, axis=1, keepdims=True)
    nb[...] = jnp.broadcast_to(row_norm, nb.shape)
    rowsm[...] = (rows * -2.0).astype(BF16)

    def kern(total):
        total = jnp.maximum(total, 1.0)
        return jnp.exp2(total * lax.rsqrt(total) * rate)

    block_tile = kern(nt(rowsm[...], blk) + (row_norm + blk_norm))
    mt = jnp.dot(block_tile, eig[...], precision=HIGHEST, preferred_element_type=F32)
    mt_loc[...] = mt.reshape(mt_loc.shape)
    send_all(1, lambda t: mt_loc.at[t], mt_recv)
    mt_recv[me] = mt_loc[me]

    acc[...] = jnp.zeros_like(acc)

    def main_b(bi, carry):
        at_b = pl.ds(pl.multiple_of(bi * step_b, step_b), step_b)

        def main_j(ji, carry):
            for sub in range(step_j // 256):
                at = pl.ds(pl.multiple_of(ji * step_j + sub * 256, 256), 256)
                norm = jnp.concatenate([nb[at_b, :]] * (256 // nb.shape[1]), axis=1)
                tile = kern(nt(rowsm[at_b, :], cen[at, :]) + (norm + nj[:1, at]))
                high, low = split(tile)
                khi[:, sub * 256:(sub + 1) * 256] = high
                klo[:, sub * 256:(sub + 1) * 256] = low
            at = pl.ds(pl.multiple_of(ji * step_j, step_j), step_j)
            acc[at_b, :] += nt(khi[...], w2[:, at]) + nt(klo[...], w2[:, at])
            return carry

        return lax.fori_loop(0, count // step_j, main_j, carry)

    lax.fori_loop(0, batch // step_b, main_b, 0)
    both = acc[:, :lanes] + acc[:, lanes:]
    p_loc[...] = jnp.sum(both.reshape(n, per, lanes) * b_mask[None], axis=1, keepdims=True)
    send_all(2, lambda t: p_loc.at[t], p_recv)
    p_recv[me] = p_loc[me]

    wait_bytes(mt_recv, recv_sems.at[1])
    mt_all[me] = jnp.sum(mt_recv[...], axis=0)
    send_all(3, lambda t: mt_all.at[me], mt_all)

    wait_bytes(p_recv, recv_sems.at[2])
    mine = jnp.sum(p_recv[...], axis=0) - tgt
    r_all[me] = mine
    send_all(4, lambda t: r_all.at[me], r_all)
    res_out[...] = nt(mine * o_mask, b_mask, HIGHEST)

    wait_bytes(mt_all, recv_sems.at[3])
    carry_n = nt(scaled, mt_all[...].reshape(batch, scaled.shape[1]), HIGHEST)
    wait_bytes(r_all, recv_sems.at[4])
    spread = (r_all[...] * b_mask[None]).reshape(batch, lanes)
    wide = jnp.dot(carry_n, spread, precision=HIGHEST, preferred_element_type=F32)
    corr_out[...] = nt(o_mask, wide, HIGHEST)

    wait_bytes(rows_buf, send_sems.at[0])
    wait_bytes(mt_loc, send_sems.at[1])
    wait_bytes(p_loc, send_sems.at[2])
    wait_bytes(mt_all, send_sems.at[3])
    wait_bytes(r_all, send_sems.at[4])


def on_device(nx, ny, centres, weights, targets, batch_index, nystrom_index, eigvecs, scales):
    n = nx * ny
    count, dim = centres.shape
    outputs = weights.shape[0]
    per = batch_index.shape[0]
    block = nystrom_index.shape[0]
    eigen = eigvecs.shape[1]
    lanes = per * outputs
    batch = n * per
    step_j = min(count, 1024)
    step_b = min(batch, 256)
    vmem = pl.BlockSpec(memory_space=pltpu.VMEM)
    hbm = pl.BlockSpec(memory_space=pl.ANY)
    return pl.pallas_call(
        functools.partial(kernel, nx, ny),
        out_shape=(
            jax.ShapeDtypeStruct((outputs, per), F32),
            jax.ShapeDtypeStruct((outputs, block), F32),
        ),
        in_specs=[vmem] * 5 + [hbm] * 2,
        out_specs=(vmem, vmem),
        scratch_shapes=[
            pltpu.VMEM((count, dim), BF16),
            pltpu.VMEM((outputs, count), F32),
            pltpu.VMEM((2 * lanes, count), BF16),
            pltpu.VMEM((8, count), F32),
            pltpu.VMEM((n, per, dim), BF16),
            pltpu.VMEM((batch, dim), BF16),
            pltpu.VMEM((batch, 128), F32),
            pltpu.VMEM((batch, 2 * lanes), F32),
            pltpu.VMEM((step_b, step_j), BF16),
            pltpu.VMEM((step_b, step_j), BF16),
            pltpu.VMEM((n, per, eigen), F32),
            pltpu.VMEM((n, per, eigen), F32),
            pltpu.VMEM((n, per, eigen), F32),
            pltpu.VMEM((n, 1, lanes), F32),
            pltpu.VMEM((n, 1, lanes), F32),
            pltpu.VMEM((n, 1, lanes), F32),
            pltpu.SemaphoreType.DMA((4,)),
            pltpu.SemaphoreType.DMA,
            pltpu.SemaphoreType.DMA((5,)),
            pltpu.SemaphoreType.DMA((5,)),
        ],
        compiler_params=pltpu.CompilerParams(
            collective_id=0, has_side_effects=True, vmem_limit_bytes=60 * 1024 * 1024
        ),
    )(
        batch_index.reshape(1, per), nystrom_index.reshape(1, block), targets, eigvecs,
        scales.reshape(1, eigen), weights, centres,
    )


def solution(mesh):
    return jax.shard_map(
        functools.partial(on_device, mesh.shape["gx"], mesh.shape["gy"]),
        mesh=mesh,
        in_specs=(
            P(("gx", "gy"), None),
            P(None, ("gx", "gy")),
            P(None, ("gx", "gy")),
            P(("gx", "gy")),
            P(("gx", "gy")),
            P(("gx", "gy"), None),
            P(),
        ),
        out_specs=(P(None, ("gx", "gy")), P(None, ("gx", "gy"))),
        check_vma=False,
    )
```

```python
import functools
import math

import jax
import jax.numpy as jnp
from jax import lax
from jax.experimental import pallas as pl
from jax.experimental.pallas import tpu as pltpu
from jax.sharding import PartitionSpec as P

F32 = jnp.float32
BF16 = jnp.bfloat16
HIGHEST = lax.Precision.HIGHEST
NT = (((1,), (1,)), ((), ()))
MESH = pl.DeviceIdType.MESH


def nt(a, b, precision=None):
    return lax.dot_general(a, b, NT, precision=precision, preferred_element_type=F32)


def split(x):
    high = x.astype(BF16)
    return high, (x - high.astype(F32)).astype(BF16)


def kernel(
    nx, ny,
    bidx, nidx, targets, eig, scales, weights_hbm, centres_hbm,
    res_out, corr_out,
    cen, wv, w2, nj, rows_buf, rowsm, nb, acc, khi, klo,
    mt_loc, mt_recv, mt_all, p_loc, p_recv, r_all,
    cen_sem, w_sem, send_sems, recv_sems,
):
    n = nx * ny
    gx, gy = lax.axis_index("gx"), lax.axis_index("gy")
    me = gx * ny + gy
    count, dim = cen.shape
    outputs = wv.shape[0]
    per = rows_buf.shape[1]
    batch = n * per
    lanes = per * outputs
    block = eig.shape[0]
    step_j = khi.shape[1]
    step_b = khi.shape[0]
    rate = -math.log2(math.e) / float(dim) ** 0.5

    cen_copies = []
    parts = cen_sem.shape[0]
    size = count // parts
    for part in range(parts):
        at = pl.ds(part * size, size)
        copy = pltpu.make_async_copy(centres_hbm.at[at], cen.at[at], cen_sem.at[part])
        copy.start()
        cen_copies.append(copy)
    w_copy = pltpu.make_async_copy(weights_hbm, wv, w_sem)
    w_copy.start()

    barrier = pltpu.get_barrier_semaphore()

    def other(k):
        t = lax.rem(me + k, n)
        return t, (lax.div(t, ny), lax.rem(t, ny))

    def greet(k, carry):
        _, where = other(k)
        pl.semaphore_signal(barrier, inc=1, device_id=where, device_id_type=MESH)
        return carry

    lax.fori_loop(1, n, greet, 0)

    def send_all(phase, source, target):
        def one(k, carry):
            t, where = other(k)
            pltpu.make_async_remote_copy(
                src_ref=source(t), dst_ref=target.at[me],
                send_sem=send_sems.at[phase], recv_sem=recv_sems.at[phase],
                device_id=where, device_id_type=MESH,
            ).start()
            return carry

        lax.fori_loop(1, n, one, 0)

    def wait_bytes(buf, sem):
        view = buf.at[pl.ds(0, n - 1)]
        pltpu.make_async_copy(view, view, sem).wait()

    first = me * count

    def column(ref):
        length = ref.shape[1]
        local = (ref[...] - first).astype(F32)
        row = lax.broadcasted_iota(jnp.int32, (length, length), 0)
        col = lax.broadcasted_iota(jnp.int32, (length, length), 1)
        return jnp.sum(jnp.where(row == col, local, 0.0), axis=1, keepdims=True)

    wanted = jnp.concatenate([column(bidx), column(nidx)], axis=0)
    picked = jnp.zeros((per + block, dim), F32)
    for part in range(parts):
        cen_copies[part].wait()
        spot = lax.broadcasted_iota(jnp.int32, (per + block, size), 1) + part * size
        hot = jnp.where(spot.astype(F32) == wanted, 1.0, 0.0).astype(BF16)
        picked = picked + jnp.dot(hot, cen[part * size:(part + 1) * size, :], preferred_element_type=F32)
    rows_buf[me] = picked[:per].astype(BF16)
    pl.semaphore_wait(barrier, n - 1)
    send_all(0, lambda t: rows_buf.at[me], rows_buf)

    blk = picked[per:]
    ones_f = jnp.ones((8, dim), F32)
    blk_norm = nt(ones_f, blk * blk, HIGHEST)[:1]
    blk = blk.astype(BF16)
    ones_b = jnp.ones((8, dim), BF16)

    def norms(i, carry):
        at = pl.ds(pl.multiple_of(i * 512, 512), 512)
        v = cen[at, :].astype(F32)
        high, low = split(v * v)
        nj[:, at] = nt(ones_b, high) + nt(ones_b, low)
        return carry

    lax.fori_loop(0, count // 512, norms, 0)
    w_copy.wait()
    whigh, wlow = split(wv[...])
    for rep in range(per):
        w2[rep * outputs:(rep + 1) * outputs, :] = whigh
        w2[lanes + rep * outputs:lanes + (rep + 1) * outputs, :] = wlow
    scaled = eig[...] * scales[...]
    o_row = lax.broadcasted_iota(jnp.int32, (outputs, lanes), 0)
    o_col = lax.broadcasted_iota(jnp.int32, (outputs, lanes), 1)
    o_mask = jnp.where(lax.rem(o_col, outputs) == o_row, 1.0, 0.0)
    b_row = lax.broadcasted_iota(jnp.int32, (per, lanes), 0)
    b_col = lax.broadcasted_iota(jnp.int32, (per, lanes), 1)
    b_mask = jnp.where(lax.div(b_col, outputs) == b_row, 1.0, 0.0)
    tgt = jnp.dot(targets[...], o_mask, precision=HIGHEST, preferred_element_type=F32)
    tgt = jnp.sum(tgt * b_mask, axis=0, keepdims=True)

    wait_bytes(rows_buf, recv_sems.at[0])
    rows = rows_buf[...].astype(F32).reshape(batch, dim)
    row_norm = jnp.sum(rows * rows, axis=1, keepdims=True)
    nb[...] = jnp.broadcast_to(row_norm, nb.shape)
    rowsm[...] = (rows * -2.0).astype(BF16)

    def kern(total):
        total = jnp.maximum(total, 1.0)
        return jnp.exp2(total * lax.rsqrt(total) * rate)

    block_tile = kern(nt(rowsm[...], blk) + (row_norm + blk_norm))
    mt = jnp.dot(block_tile, eig[...], precision=HIGHEST, preferred_element_type=F32)
    mt_loc[...] = mt.reshape(mt_loc.shape)
    send_all(1, lambda t: mt_loc.at[t], mt_recv)
    mt_recv[me] = mt_loc[me]

    acc[...] = jnp.zeros_like(acc)

    def main_b(bi, carry):
        at_b = pl.ds(pl.multiple_of(bi * step_b, step_b), step_b)

        def main_j(ji, carry):
            for sub in range(step_j // 256):
                at = pl.ds(pl.multiple_of(ji * step_j + sub * 256, 256), 256)
                norm = jnp.concatenate([nb[at_b, :]] * (256 // nb.shape[1]), axis=1)
                tile = kern(nt(rowsm[at_b, :], cen[at, :]) + (norm + nj[:1, at]))
                high, low = split(tile)
                khi[:, sub * 256:(sub + 1) * 256] = high
                klo[:, sub * 256:(sub + 1) * 256] = low
            at = pl.ds(pl.multiple_of(ji * step_j, step_j), step_j)
            acc[at_b, :] += nt(khi[...], w2[:, at]) + nt(klo[...], w2[:, at])
            return carry

        return lax.fori_loop(0, count // step_j, main_j, carry)

    lax.fori_loop(0, batch // step_b, main_b, 0)
    both = acc[:, :lanes] + acc[:, lanes:]
    p_loc[...] = jnp.sum(both.reshape(n, per, lanes) * b_mask[None], axis=1, keepdims=True)
    send_all(2, lambda t: p_loc.at[t], p_recv)
    p_recv[me] = p_loc[me]

    wait_bytes(mt_recv, recv_sems.at[1])
    mt_all[me] = jnp.sum(mt_recv[...], axis=0)
    send_all(3, lambda t: mt_all.at[me], mt_all)

    wait_bytes(p_recv, recv_sems.at[2])
    mine = jnp.sum(p_recv[...], axis=0) - tgt
    r_all[me] = mine
    send_all(4, lambda t: r_all.at[me], r_all)
    res_out[...] = nt(mine * b_mask, o_mask, HIGHEST)

    wait_bytes(mt_all, recv_sems.at[3])
    carry_n = nt(scaled, mt_all[...].reshape(batch, scaled.shape[1]), HIGHEST)
    wait_bytes(r_all, recv_sems.at[4])
    spread = (r_all[...] * b_mask[None]).reshape(batch, lanes)
    wide = jnp.dot(carry_n, spread, precision=HIGHEST, preferred_element_type=F32)
    corr_out[...] = nt(o_mask, wide, HIGHEST)

    wait_bytes(rows_buf, send_sems.at[0])
    wait_bytes(mt_loc, send_sems.at[1])
    wait_bytes(p_loc, send_sems.at[2])
    wait_bytes(mt_all, send_sems.at[3])
    wait_bytes(r_all, send_sems.at[4])


def hand_out(res_in, corr_in, res_out, corr_out):
    res_out[...] = res_in[...]
    corr_out[...] = corr_in[...]


def on_device(nx, ny, centres, weights, targets, batch_index, nystrom_index, eigvecs, scales):
    n = nx * ny
    count, dim = centres.shape
    outputs = weights.shape[0]
    per = batch_index.shape[0]
    block = nystrom_index.shape[0]
    eigen = eigvecs.shape[1]
    lanes = per * outputs
    batch = n * per
    step_j = min(count, 1024)
    step_b = min(batch, 256)
    vmem = pl.BlockSpec(memory_space=pltpu.VMEM)
    hbm = pl.BlockSpec(memory_space=pl.ANY)
    res, corr = pl.pallas_call(
        functools.partial(kernel, nx, ny),
        out_shape=(
            jax.ShapeDtypeStruct((per, outputs), F32),
            jax.ShapeDtypeStruct((outputs, block), F32),
        ),
        in_specs=[vmem] * 5 + [hbm] * 2,
        out_specs=(vmem, vmem),
        scratch_shapes=[
            pltpu.VMEM((count, dim), BF16),
            pltpu.VMEM((outputs, count), F32),
            pltpu.VMEM((2 * lanes, count), BF16),
            pltpu.VMEM((8, count), F32),
            pltpu.VMEM((n, per, dim), BF16),
            pltpu.VMEM((batch, dim), BF16),
            pltpu.VMEM((batch, 128), F32),
            pltpu.VMEM((batch, 2 * lanes), F32),
            pltpu.VMEM((step_b, step_j), BF16),
            pltpu.VMEM((step_b, step_j), BF16),
            pltpu.VMEM((n, per, eigen), F32),
            pltpu.VMEM((n, per, eigen), F32),
            pltpu.VMEM((n, per, eigen), F32),
            pltpu.VMEM((n, 1, lanes), F32),
            pltpu.VMEM((n, 1, lanes), F32),
            pltpu.VMEM((n, 1, lanes), F32),
            pltpu.SemaphoreType.DMA((4,)),
            pltpu.SemaphoreType.DMA,
            pltpu.SemaphoreType.DMA((5,)),
            pltpu.SemaphoreType.DMA((5,)),
        ],
        compiler_params=pltpu.CompilerParams(
            collective_id=0, has_side_effects=True, vmem_limit_bytes=60 * 1024 * 1024
        ),
    )(
        batch_index.reshape(1, per), nystrom_index.reshape(1, block), targets.T, eigvecs,
        scales.reshape(1, eigen), weights, centres,
    )
    res, corr = pl.pallas_call(
        hand_out,
        out_shape=(jax.ShapeDtypeStruct(res.shape, F32), jax.ShapeDtypeStruct(corr.shape, F32)),
        in_specs=[vmem] * 2,
        out_specs=(vmem, vmem),
    )(res, corr)
    return res.T, corr


def solution(mesh):
    return jax.shard_map(
        functools.partial(on_device, mesh.shape["gx"], mesh.shape["gy"]),
        mesh=mesh,
        in_specs=(
            P(("gx", "gy"), None),
            P(None, ("gx", "gy")),
            P(None, ("gx", "gy")),
            P(("gx", "gy")),
            P(("gx", "gy")),
            P(("gx", "gy"), None),
            P(),
        ),
        out_specs=(P(None, ("gx", "gy")), P(None, ("gx", "gy"))),
        check_vma=False,
    )
```

```python
import functools
import math

import jax
import jax.numpy as jnp
from jax import lax
from jax.experimental import pallas as pl
from jax.experimental.pallas import tpu as pltpu
from jax.sharding import PartitionSpec as P

F32 = jnp.float32
BF16 = jnp.bfloat16
HIGHEST = lax.Precision.HIGHEST
NT = (((1,), (1,)), ((), ()))
MESH = pl.DeviceIdType.MESH


def nt(a, b, precision=None):
    return lax.dot_general(a, b, NT, precision=precision, preferred_element_type=F32)


def split(x):
    high = x.astype(BF16)
    return high, (x - high.astype(F32)).astype(BF16)


def kernel(
    nx, ny,
    bidx, nidx, targets, eig, scales, weights_hbm, centres_hbm,
    res_out, corr_out,
    cen, wv, w2, nj, rows_buf, rowsm, nb, acc, khi,
    mt_loc, mt_recv, mt_all, p_loc, p_recv, r_all,
    cen_sem, w_sem, send_sems, recv_sems,
):
    n = nx * ny
    gx, gy = lax.axis_index("gx"), lax.axis_index("gy")
    me = gx * ny + gy
    count, dim = cen.shape
    outputs = wv.shape[0]
    per = rows_buf.shape[1]
    batch = n * per
    lanes = per * outputs
    block = eig.shape[0]
    step_j = khi.shape[1]
    step_b = khi.shape[0] // 2
    rate = -math.log2(math.e) / float(dim) ** 0.5

    cen_copies = []
    parts = cen_sem.shape[0]
    size = count // parts
    for part in range(parts):
        at = pl.ds(part * size, size)
        copy = pltpu.make_async_copy(centres_hbm.at[at], cen.at[at], cen_sem.at[part])
        copy.start()
        cen_copies.append(copy)
    w_copy = pltpu.make_async_copy(weights_hbm, wv, w_sem)
    w_copy.start()

    barrier = pltpu.get_barrier_semaphore()

    def other(k):
        t = lax.rem(me + k, n)
        return t, (lax.div(t, ny), lax.rem(t, ny))

    def greet(k, carry):
        _, where = other(k)
        pl.semaphore_signal(barrier, inc=1, device_id=where, device_id_type=MESH)
        return carry

    lax.fori_loop(1, n, greet, 0)

    def send_all(phase, source, target):
        def one(k, carry):
            t, where = other(k)
            pltpu.make_async_remote_copy(
                src_ref=source(t), dst_ref=target.at[me],
                send_sem=send_sems.at[phase], recv_sem=recv_sems.at[phase],
                device_id=where, device_id_type=MESH,
            ).start()
            return carry

        lax.fori_loop(1, n, one, 0)

    def wait_bytes(buf, sem):
        view = buf.at[pl.ds(0, n - 1)]
        pltpu.make_async_copy(view, view, sem).wait()

    first = me * count

    def column(ref):
        length = ref.shape[1]
        local = (ref[...] - first).astype(F32)
        row = lax.broadcasted_iota(jnp.int32, (length, length), 0)
        col = lax.broadcasted_iota(jnp.int32, (length, length), 1)
        return jnp.sum(jnp.where(row == col, local, 0.0), axis=1, keepdims=True)

    wanted = jnp.concatenate([column(bidx), column(nidx)], axis=0)
    picked = jnp.zeros((per + block, dim), F32)
    for part in range(parts):
        cen_copies[part].wait()
        spot = lax.broadcasted_iota(jnp.int32, (per + block, size), 1) + part * size
        hot = jnp.where(spot.astype(F32) == wanted, 1.0, 0.0).astype(BF16)
        picked = picked + jnp.dot(hot, cen[part * size:(part + 1) * size, :], preferred_element_type=F32)
    rows_buf[me] = picked[:per].astype(BF16)
    pl.semaphore_wait(barrier, n - 1)
    send_all(0, lambda t: rows_buf.at[me], rows_buf)

    blk = picked[per:]
    ones_f = jnp.ones((8, dim), F32)
    blk_norm = nt(ones_f, blk * blk, HIGHEST)[:1]
    blk = blk.astype(BF16)
    ones_b = jnp.ones((8, dim), BF16)

    def norms(i, carry):
        at = pl.ds(pl.multiple_of(i * 512, 512), 512)
        v = cen[at, :].astype(F32)
        high, low = split(v * v)
        nj[:, at] = nt(ones_b, high) + nt(ones_b, low)
        return carry

    lax.fori_loop(0, count // 512, norms, 0)
    w_copy.wait()
    whigh, wlow = split(wv[...])
    for rep in range(per):
        w2[rep * outputs:(rep + 1) * outputs, :] = whigh
        w2[lanes + rep * outputs:lanes + (rep + 1) * outputs, :] = wlow
    scaled = eig[...] * scales[...]
    o_row = lax.broadcasted_iota(jnp.int32, (outputs, lanes), 0)
    o_col = lax.broadcasted_iota(jnp.int32, (outputs, lanes), 1)
    o_mask = jnp.where(lax.rem(o_col, outputs) == o_row, 1.0, 0.0)
    b_row = lax.broadcasted_iota(jnp.int32, (per, lanes), 0)
    b_col = lax.broadcasted_iota(jnp.int32, (per, lanes), 1)
    b_mask = jnp.where(lax.div(b_col, outputs) == b_row, 1.0, 0.0)
    tgt = jnp.dot(targets[...], o_mask, precision=HIGHEST, preferred_element_type=F32)
    tgt = jnp.sum(tgt * b_mask, axis=0, keepdims=True)

    wait_bytes(rows_buf, recv_sems.at[0])
    rows = rows_buf[...].astype(F32).reshape(batch, dim)
    row_norm = jnp.sum(rows * rows, axis=1, keepdims=True)
    nb[...] = jnp.broadcast_to(row_norm, nb.shape)
    rowsm[...] = (rows * -2.0).astype(BF16)

    def kern(total):
        total = jnp.maximum(total, 1.0)
        return jnp.exp2(total * lax.rsqrt(total) * rate)

    block_tile = kern(nt(rowsm[...], blk) + (row_norm + blk_norm))
    mt = jnp.dot(block_tile, eig[...], precision=HIGHEST, preferred_element_type=F32)
    mt_loc[...] = mt.reshape(mt_loc.shape)
    send_all(1, lambda t: mt_loc.at[t], mt_recv)
    mt_recv[me] = mt_loc[me]

    acc[...] = jnp.zeros_like(acc)

    def main_b(bi, carry):
        at_b = pl.ds(pl.multiple_of(bi * step_b, step_b), step_b)

        def main_j(ji, carry):
            for sub in range(step_j // 256):
                at = pl.ds(pl.multiple_of(ji * step_j + sub * 256, 256), 256)
                norm = jnp.concatenate([nb[at_b, :]] * (256 // nb.shape[1]), axis=1)
                tile = kern(nt(rowsm[at_b, :], cen[at, :]) + (norm + nj[:1, at]))
                high, low = split(tile)
                khi[:step_b, sub * 256:(sub + 1) * 256] = high
                khi[step_b:, sub * 256:(sub + 1) * 256] = low
            at = pl.ds(pl.multiple_of(ji * step_j, step_j), step_j)
            terms = nt(khi[...], w2[:, at])
            acc[at_b, :] += terms[:step_b] + terms[step_b:]
            return carry

        return lax.fori_loop(0, count // step_j, main_j, carry)

    lax.fori_loop(0, batch // step_b, main_b, 0)
    both = acc[:, :lanes] + acc[:, lanes:]
    p_loc[...] = jnp.sum(both.reshape(n, per, lanes) * b_mask[None], axis=1, keepdims=True)
    send_all(2, lambda t: p_loc.at[t], p_recv)
    p_recv[me] = p_loc[me]

    wait_bytes(mt_recv, recv_sems.at[1])
    mt_all[me] = jnp.sum(mt_recv[...], axis=0)
    send_all(3, lambda t: mt_all.at[me], mt_all)

    wait_bytes(p_recv, recv_sems.at[2])
    mine = jnp.sum(p_recv[...], axis=0) - tgt
    r_all[me] = mine
    send_all(4, lambda t: r_all.at[me], r_all)
    res_out[...] = nt(mine * b_mask, o_mask, HIGHEST)

    wait_bytes(mt_all, recv_sems.at[3])
    carry_n = nt(scaled, mt_all[...].reshape(batch, scaled.shape[1]), HIGHEST)
    wait_bytes(r_all, recv_sems.at[4])
    spread = (r_all[...] * b_mask[None]).reshape(batch, lanes)
    wide = jnp.dot(carry_n, spread, precision=HIGHEST, preferred_element_type=F32)
    corr_out[...] = nt(o_mask, wide, HIGHEST)

    wait_bytes(rows_buf, send_sems.at[0])
    wait_bytes(mt_loc, send_sems.at[1])
    wait_bytes(p_loc, send_sems.at[2])
    wait_bytes(mt_all, send_sems.at[3])
    wait_bytes(r_all, send_sems.at[4])


def hand_out(res_in, corr_in, res_out, corr_out):
    res_out[...] = res_in[...]
    corr_out[...] = corr_in[...]


def on_device(nx, ny, centres, weights, targets, batch_index, nystrom_index, eigvecs, scales):
    n = nx * ny
    count, dim = centres.shape
    outputs = weights.shape[0]
    per = batch_index.shape[0]
    block = nystrom_index.shape[0]
    eigen = eigvecs.shape[1]
    lanes = per * outputs
    batch = n * per
    step_j = min(count, 4096)
    step_b = min(batch, 256)
    vmem = pl.BlockSpec(memory_space=pltpu.VMEM)
    hbm = pl.BlockSpec(memory_space=pl.ANY)
    res, corr = pl.pallas_call(
        functools.partial(kernel, nx, ny),
        out_shape=(
            jax.ShapeDtypeStruct((per, outputs), F32),
            jax.ShapeDtypeStruct((outputs, block), F32),
        ),
        in_specs=[vmem] * 5 + [hbm] * 2,
        out_specs=(vmem, vmem),
        scratch_shapes=[
            pltpu.VMEM((count, dim), BF16),
            pltpu.VMEM((outputs, count), F32),
            pltpu.VMEM((2 * lanes, count), BF16),
            pltpu.VMEM((8, count), F32),
            pltpu.VMEM((n, per, dim), BF16),
            pltpu.VMEM((batch, dim), BF16),
            pltpu.VMEM((batch, 128), F32),
            pltpu.VMEM((batch, 2 * lanes), F32),
            pltpu.VMEM((2 * step_b, step_j), BF16),
            pltpu.VMEM((n, per, eigen), F32),
            pltpu.VMEM((n, per, eigen), F32),
            pltpu.VMEM((n, per, eigen), F32),
            pltpu.VMEM((n, 1, lanes), F32),
            pltpu.VMEM((n, 1, lanes), F32),
            pltpu.VMEM((n, 1, lanes), F32),
            pltpu.SemaphoreType.DMA((4,)),
            pltpu.SemaphoreType.DMA,
            pltpu.SemaphoreType.DMA((5,)),
            pltpu.SemaphoreType.DMA((5,)),
        ],
        compiler_params=pltpu.CompilerParams(
            collective_id=0, has_side_effects=True, vmem_limit_bytes=60 * 1024 * 1024
        ),
    )(
        batch_index.reshape(1, per), nystrom_index.reshape(1, block), targets.T, eigvecs,
        scales.reshape(1, eigen), weights, centres,
    )
    res, corr = pl.pallas_call(
        hand_out,
        out_shape=(jax.ShapeDtypeStruct(res.shape, F32), jax.ShapeDtypeStruct(corr.shape, F32)),
        in_specs=[vmem] * 2,
        out_specs=(vmem, vmem),
    )(res, corr)
    return res.T, corr


def solution(mesh):
    return jax.shard_map(
        functools.partial(on_device, mesh.shape["gx"], mesh.shape["gy"]),
        mesh=mesh,
        in_specs=(
            P(("gx", "gy"), None),
            P(None, ("gx", "gy")),
            P(None, ("gx", "gy")),
            P(("gx", "gy")),
            P(("gx", "gy")),
            P(("gx", "gy"), None),
            P(),
        ),
        out_specs=(P(None, ("gx", "gy")), P(None, ("gx", "gy"))),
        check_vma=False,
    )
```
